256 devices in a mesh: gy: 4 (over x), gx: 4 (over z_hi), ga: 16 (over y, z_lo, core).
Axes of the slice: x: 4, y: 4, z: 8 (z_hi: 4, z_lo: 2; z = z_hi * 2 + z_lo), core: 2. Of those that a mesh axis runs over, the one named last changes fastest.
Arguments:
- volume: bfloat16 [16, 56, 56, 7, 768], P('ga', 'gy', 'gx'), may hold values from -6 to 6
- affinity: bfloat16 [16, 3, 56, 56, 7], P('ga', None, 'gy', 'gx'), may hold values from 0 to 1
- window_dest: int32 [16, 4, 4, 4], P('ga', 'gy', 'gx'), may hold values from 0 to 16, as said below
- qkv_weight: bfloat16 [768, 1152], replicated
- proj_weight: bfloat16 [384, 768], replicated, may hold values from -0.3125 to 0.3125
- head_weight: bfloat16 [768, 3], replicated, may hold values from -0.21875 to 0.21875
Outputs:
- grad_volume: bfloat16 [16, 56, 56, 7, 768], P('ga', 'gy', 'gx')
- grad_qkv: float32 [768, 1152], P('ga')
- grad_proj: float32 [384, 768], P(None, 'ga')
The draws below stay inside these ranges and needn't reach their ends.
Inputs may be any that keep to these rules, and one draw needn't show every extreme that they name: `window_dest`: 16 marks an empty window; any other value names the device along ga, with the same gy and gx, that computes the window: the device itself or one of the min(2, 15) devices after it, cyclically (index plus 1, plus 2, modulo 16). Every device computes exactly 2 live windows, receives at most 1 from any one device, and in every group some device has 4 live windows (all of its windows), keeps 2 of them and sends 1 to each of the 2 devices after it along ga.
All inputs are finite; a program needn't handle non-finite values.
Results may differ from the reference program's by a relative error of at most 0.0065.
The reference program's roundings to bfloat16 on the way count: a program that leaves them out, or rounds other values in their place, can miss the bound.
Values may be sent and summed in bfloat16 or wider, within the bound.
No kernel may reach another device: no remote copies, remote signals or barrier semaphores. Data moves between devices by JAX's collectives and lax.ppermute only.
A program may use at most 128 MiB of HBM per device.

```python
import jax
import jax.numpy as jnp
from jax import lax

D = 768
HEADS = 12
HEAD = 32
WIN = 7
HOPS = 2
XW = 2
YW = 2
WZ = 1
CROPS = 16
WIN_DEV = 4
BAL = 2
SLOTS = 1
HDIM = 384
NX = 56
NY = 56
NZ = 7
LIVE = 175616
N_GY = 4
N_GX = 4
N_GA = 16


def draw_window_dest(key, part):
    groups = N_GY * N_GX
    reach = min(HOPS, N_GA - 1)
    low_flow = (SLOTS + 1) // 2

    def one_group(group_key):
        heavy_key, flow_key, perm_key = jax.random.split(group_key, 3)
        heavy = jax.random.randint(heavy_key, (), 0, N_GA)
        flows = jax.random.randint(flow_key, (N_GA, HOPS), low_flow, SLOTS + 1)
        sender = jnp.arange(N_GA, dtype=jnp.int32)
        column = jnp.arange(HOPS, dtype=jnp.int32)
        active = (column < reach).astype(jnp.int32)
        flows = flows * active[None, :]
        flows = jnp.where(sender[:, None] == heavy, SLOTS * active[None, :], flows)
        for offset in range(1, reach + 1):
            flows = flows.at[(heavy - offset) % N_GA, offset - 1].set(0)
        inbound = jnp.zeros((N_GA,), jnp.int32)
        for offset in range(1, reach + 1):
            inbound = inbound + jnp.roll(flows[:, offset - 1], offset)
        kept = BAL - inbound
        position = jnp.arange(WIN_DEV, dtype=jnp.int32)[None, :]
        bound = kept[:, None]
        labels = jnp.where(position < bound, sender[:, None], N_GA)
        for offset in range(1, reach + 1):
            upper = bound + flows[:, offset - 1][:, None]
            labels = jnp.where((position >= bound) & (position < upper), (sender[:, None] + offset) % N_GA, labels)
            bound = upper
        perm_keys = jax.random.split(perm_key, N_GA)
        orders = jax.vmap(lambda k: jax.random.permutation(k, WIN_DEV))(perm_keys)
        return jnp.take_along_axis(labels, orders, axis=1)
    keys_all = jax.random.split(key, groups)
    drawn = jax.vmap(one_group)(keys_all)
    return drawn.reshape(N_GY, N_GX, N_GA, WIN_DEV).transpose(2, 0, 1, 3).astype(jnp.int32)


def draw_qkv_weight(key, part):
    inner_width = HEADS * HEAD
    base = jax.random.normal(key, (D, 3 * inner_width), jnp.float32) * D ** (-0.5)
    return base.astype(jnp.bfloat16)


def block_levels(key, dims, cuts, smallest, high):
    factor_of = 1.0
    for axis_at, parts in cuts:
        heights = jax.random.uniform(jax.random.fold_in(jax.random.fold_in(key, 6), axis_at), (parts,), jnp.float32, smallest / len(cuts), high / len(cuts))
        factor_of = factor_of * jnp.repeat(jnp.exp(heights), dims[axis_at] // parts).reshape((-1,) + (1,) * (len(dims) - 1 - axis_at))
    return factor_of


def normal_values(own_key, shape, deviation, limit, pieces=(), held_as=jnp.bfloat16):
    result = jax.random.normal(own_key, shape, jnp.float32) * deviation
    if len(pieces) > 0:
        result = block_levels(own_key, shape, pieces, -0.22, 0.18) * result
    return jnp.clip(result, min=-limit, max=limit).astype(held_as)


def setup_inputs(seed: int = 0) -> dict:
    splits = jax.random.split(jax.random.key(seed), 7)
    volume = normal_values(splits[0], (CROPS, NX, NY, NZ, D), 1.0, 6.0, ((0, 16), (1, 4), (2, 4)))
    affinity = jnp.clip(1.0 * jax.random.uniform(splits[1], (CROPS, 3, NX, NY, NZ), jnp.float32) ** block_levels(splits[1], (CROPS, 3, NX, NY, NZ), ((0, 16), (2, 4), (3, 4)), -0.2, 0.2), 0.0, 1.0).astype(jnp.bfloat16)
    window_dest = draw_window_dest(jax.random.fold_in(splits[6], 71), 0)
    qkv_weight = draw_qkv_weight(jax.random.fold_in(splits[6], 71), 0)
    proj_weight = normal_values(splits[4], (HDIM, D), HDIM ** -0.5, 0.3125)
    head_weight = normal_values(splits[5], (D, 3), D ** -0.5, 0.21875)
    return {"volume": volume, "affinity": affinity, "window_dest": window_dest, "qkv_weight": qkv_weight, "proj_weight": proj_weight, "head_weight": head_weight}


LOSS_SCALE = 32.0
EPSILON = 1e-05

def window_grads(tokens, target, region, qkv_weight, proj_weight, head_weight):
    inner_width = proj_weight.shape[0]
    head_count = inner_width // HEAD
    token_count = tokens.shape[0]
    score_scale = HEAD ** (-0.5)
    floated = tokens.astype(jnp.float32)
    mean_row = lax.optimization_barrier(jnp.mean(floated, axis=-1, keepdims=True))
    centred = floated - mean_row
    variance = lax.optimization_barrier(jnp.mean(centred * centred, axis=-1, keepdims=True))
    inv_std = lax.rsqrt(variance + EPSILON)
    unit_rows = centred * inv_std
    normed = unit_rows.astype(jnp.bfloat16)
    projected = jnp.dot(normed, qkv_weight, preferred_element_type=jnp.float32).astype(jnp.bfloat16)
    projected = lax.optimization_barrier(projected).astype(jnp.float32)
    queries = projected[:, :inner_width].reshape(token_count, head_count, HEAD)
    key_rows = projected[:, inner_width:2 * inner_width].reshape(token_count, head_count, HEAD)
    values = projected[:, 2 * inner_width:].reshape(token_count, head_count, HEAD)
    scores = jnp.einsum('qhd,khd->hqk', queries, key_rows) * score_scale
    allowed = region[:, None] == region[None, :]
    scores = jnp.where(allowed[None], scores, jnp.float32(-1e+30))
    row_max = lax.optimization_barrier(jnp.max(scores, axis=-1, keepdims=True))
    exponent = jnp.exp(scores - row_max)
    attend = exponent / lax.optimization_barrier(jnp.sum(exponent, axis=-1, keepdims=True))
    attend_low = lax.optimization_barrier(attend.astype(jnp.bfloat16)).astype(jnp.float32)
    mixed = jnp.einsum('hqk,khd->qhd', attend_low, values).reshape(token_count, inner_width).astype(jnp.bfloat16)
    output = floated + jnp.dot(mixed, proj_weight, preferred_element_type=jnp.float32)
    output_low = output.astype(jnp.bfloat16)
    logits = jnp.dot(output_low, head_weight, preferred_element_type=jnp.float32)
    logit_grad = LOSS_SCALE * (jax.nn.sigmoid(logits) - target.T.astype(jnp.float32))
    output_grad = jnp.dot(logit_grad, head_weight.astype(jnp.float32).T, precision=lax.Precision.HIGHEST)
    grad_low = output_grad.astype(jnp.bfloat16)
    proj_term = jnp.dot(mixed.T, grad_low, preferred_element_type=jnp.float32)
    mixed_grad = jnp.dot(grad_low, proj_weight.T, preferred_element_type=jnp.float32).astype(jnp.bfloat16)
    mixed_grad = lax.optimization_barrier(mixed_grad).astype(jnp.float32).reshape(token_count, head_count, HEAD)
    value_grad = jnp.einsum('hqk,qhd->khd', attend_low, mixed_grad)
    attend_grad = jnp.einsum('qhd,khd->hqk', mixed_grad, values)
    score_grad = attend * (attend_grad - lax.optimization_barrier(jnp.sum(attend_grad * attend, axis=-1, keepdims=True))) * score_scale
    score_low = lax.optimization_barrier(score_grad.astype(jnp.bfloat16)).astype(jnp.float32)
    query_grad = jnp.einsum('hqk,khd->qhd', score_low, key_rows)
    key_grad = jnp.einsum('hqk,qhd->khd', score_low, queries)
    qkv_grad = jnp.concatenate([query_grad.reshape(token_count, inner_width), key_grad.reshape(token_count, inner_width), value_grad.reshape(token_count, inner_width)], axis=1).astype(jnp.bfloat16)
    qkv_term = jnp.dot(normed.T, qkv_grad, preferred_element_type=jnp.float32)
    normed_grad = jnp.dot(qkv_grad, qkv_weight.T, preferred_element_type=jnp.float32)
    grad_mean = lax.optimization_barrier(jnp.mean(normed_grad, axis=-1, keepdims=True))
    grad_along = lax.optimization_barrier(jnp.mean(normed_grad * unit_rows, axis=-1, keepdims=True))
    cell_grad = output_grad + inv_std * (normed_grad - grad_mean - unit_rows * grad_along)
    return (cell_grad.astype(jnp.bfloat16), qkv_term, proj_term)

def reference(volume, affinity, window_dest, qkv_weight, proj_weight, head_weight):
    margin = WIN // 2
    crops, size_x, size_y, size_z, width = volume.shape
    cells = WIN ** 3
    rolled = jnp.roll(volume, (-margin, -margin, -margin), axis=(1, 2, 3))
    rolled_aff = jnp.roll(affinity, (-margin, -margin, -margin), axis=(2, 3, 4))
    wins_x, wins_y, wins_z = (size_x // WIN, size_y // WIN, size_z // WIN)
    tokens = rolled.reshape(crops, wins_x, WIN, wins_y, WIN, wins_z, WIN, width).transpose(0, 1, 3, 5, 2, 4, 6, 7).reshape(-1, cells, width)
    targets = rolled_aff.reshape(crops, 3, wins_x, WIN, wins_y, WIN, wins_z, WIN).transpose(0, 2, 4, 6, 1, 3, 5, 7).reshape(-1, 3, cells)
    flag_x = (jnp.arange(size_x) >= size_x - margin).astype(jnp.int32)
    flag_y = (jnp.arange(size_y) >= size_y - margin).astype(jnp.int32)
    flag_z = (jnp.arange(size_z) >= size_z - margin).astype(jnp.int32)
    region_grid = flag_x[:, None, None] * 4 + flag_y[None, :, None] * 2 + flag_z[None, None, :]
    regions = region_grid.reshape(wins_x, WIN, wins_y, WIN, wins_z, WIN).transpose(0, 2, 4, 1, 3, 5).reshape(1, -1, cells)
    regions = jnp.broadcast_to(regions, (crops, wins_x * wins_y * wins_z, cells)).reshape(-1, cells)
    live = window_dest.reshape(crops, N_GY, N_GX, XW, YW, WZ).transpose(0, 1, 3, 2, 4, 5).reshape(-1) < N_GA

    def step(carry, item):
        tok, tgt, reg, flag = item

        def compute(operands):
            return window_grads(operands[0], operands[1], operands[2], qkv_weight, proj_weight, head_weight)

        def skip(operands):
            return (jnp.zeros((cells, width), jnp.bfloat16), jnp.zeros(qkv_weight.shape, jnp.float32), jnp.zeros(proj_weight.shape, jnp.float32))
        cell_grad, qkv_term, proj_term = lax.cond(flag, compute, skip, (tok, tgt, reg))
        return ((carry[0] + qkv_term, carry[1] + proj_term), cell_grad)
    start = (jnp.zeros(qkv_weight.shape, jnp.float32), jnp.zeros(proj_weight.shape, jnp.float32))
    (total_qkv, total_proj), window_grad = lax.scan(step, start, (tokens, targets, regions, live))
    grid = window_grad.reshape(crops, wins_x, wins_y, wins_z, WIN, WIN, WIN, width).transpose(0, 1, 4, 2, 5, 3, 6, 7).reshape(crops, size_x, size_y, size_z, width)
    grad_volume = jnp.roll(grid, (margin, margin, margin), axis=(1, 2, 3))
    factor = float(LIVE) ** (-0.5)
    return (grad_volume, total_qkv * factor, total_proj * factor)
```

```python
import functools

import jax
import jax.numpy as jnp
import numpy as np
from jax import lax
from jax.experimental import pallas as pl
from jax.experimental.pallas import tpu as pltpu
from jax.sharding import PartitionSpec as P


HEAD = 32
WIN = 7
MARGIN = 3
LOSS_SCALE = 32.0
EPSILON = 1e-05
LOW_CELLS = 147
HIGH_CELLS = 196
LOW_ROWS = 160
HIGH_ROWS = 208
ROWS = LOW_ROWS + HIGH_ROWS
BLOCKS = ((0, LOW_ROWS, LOW_CELLS), (LOW_ROWS, HIGH_ROWS, HIGH_CELLS))
GROUP = 128
PER_GROUP = GROUP // HEAD
MASKED = -1e30
RIM_ROWS = 240
CORNER_ROWS = 64
LOW_Z = 3
OUTER = 4
F32 = jnp.float32
BF16 = jnp.bfloat16


def mm(a, b):
    return lax.dot_general(a, b, (((1,), (0,)), ((), ())), preferred_element_type=F32)


def mm_nt(a, b):
    return lax.dot_general(a, b, (((1,), (1,)), ((), ())), preferred_element_type=F32)


def row_cells():
    cells = np.full((ROWS, 3), -1)
    for z in range(WIN):
        for x in range(WIN):
            for y in range(WIN):
                if z < LOW_Z:
                    row = z * 49 + x * WIN + y
                else:
                    row = LOW_ROWS + (z - LOW_Z) * 49 + x * WIN + y
                cells[row] = (x, y, z)
    return cells


def source_rows():
    rest = 2 * WIN - MARGIN
    table = np.full((4, ROWS), -1)
    for row, (x, y, z) in enumerate(row_cells()):
        if x < 0:
            continue
        table[0, row] = (x * WIN + y) * 8 + z
        if y < OUTER:
            table[1, row] = (x * OUTER + y) * 8 + z
        else:
            table[1, row] = 224 + (x * MARGIN + y - OUTER) * WIN + z
        if x < OUTER:
            table[2, row] = (x * WIN + y) * 8 + z
        else:
            table[2, row] = 224 + ((x - OUTER) * rest + y) * WIN + z
        if x < OUTER and y < OUTER:
            table[3, row] = (x * OUTER + y) * 8 + z
        elif x < OUTER:
            table[3, row] = 128 + ((x + WIN) * MARGIN + y - OUTER) * WIN + z - 144
        elif y < OUTER:
            table[3, row] = 224 + ((x - OUTER) * rest + y + WIN) * WIN + z - 48
        else:
            table[3, row] = 416 + ((x - OUTER) * MARGIN + y - OUTER) * WIN + z
    table = np.pad(table, ((0, 0), (0, 3 * GROUP - ROWS)), constant_values=-1)
    return np.repeat(table[:, None, :], 8, axis=1).astype(np.float32)


def grid_rows():
    table = np.full((8, ROWS), -1)
    for row, (x, y, z) in enumerate(row_cells()):
        if x >= 0:
            table[:, row] = (x * WIN + y) * 8 + z
    return table.astype(np.int32)


def edge_code(index, edge_x, edge_y):
    by_row = jnp.floor((index + 0.5) * (1.0 / 7.0))
    y = index - 7.0 * by_row
    z = jnp.floor((by_row + 0.5) * (1.0 / 7.0))
    x = by_row - 7.0 * z
    on_x = jnp.where(x >= 4.0, edge_x, 0.0)
    on_y = jnp.where(y >= 4.0, edge_y, 0.0)
    return 2.0 * on_x + on_y


def head_masks():
    lane = lax.broadcasted_iota(jnp.int32, (1, GROUP), 1)
    return [
        jnp.where((lane >= h * HEAD) & (lane < (h + 1) * HEAD), 1.0, 0.0).astype(BF16)
        for h in range(PER_GROUP)
    ]


def take_own(vol_ref, aff_ref, own, xs, ys):
    count = len(xs) * len(ys)
    width = vol_ref.shape[-1]
    for i, x in enumerate(xs):
        at = slice(i * len(ys), (i + 1) * len(ys))
        own[at, 0:WIN, 0:width] = vol_ref[x, ys[0] : ys[-1] + 1].astype(F32)
        own[at, 0:WIN, width:] = aff_ref[x, ys[0] : ys[-1] + 1].astype(F32)
    rows = count * 8
    return own[0:count].reshape(rows, own.shape[-1]).astype(BF16)


def gather_rows(index, sources):
    depth = sources.shape[0]
    at = lax.broadcasted_iota(jnp.int32, (ROWS, depth), 1)
    column = index.T[:ROWS, 0:1].astype(jnp.int32)
    chosen = jnp.where(column == at, 1.0, 0.0).astype(BF16)
    return mm(chosen, sources)


def window_terms(info, window, cells, weights, outs, acc_q, acc_p, scratch):
    wqkv_ref, proj_ref, headt_ref = weights
    tok_ref, lg_ref, d_ref = outs
    qkv_s, mixed_s, mg_s, p_low, p_high, bias_low, bias_high = scratch
    inner, width = proj_ref.shape
    groups = inner // GROUP
    scale = HEAD ** (-0.5)
    p_refs = (p_low, p_high)
    bias_refs = (bias_low, bias_high)
    edge_x = jnp.where((info[4] != 0) & (window >= 2), 1.0, 0.0)
    edge_y = jnp.where((info[5] != 0) & (lax.rem(window, 2) == 1), 1.0, 0.0)
    for (_, rows, cells_here), bias in zip(BLOCKS, bias_refs):
        down = lax.broadcasted_iota(jnp.int32, (rows, 1), 0).astype(F32)
        along = lax.broadcasted_iota(jnp.int32, (1, rows), 1).astype(F32)
        same = edge_code(down, edge_x, edge_y) == edge_code(along, edge_x, edge_y)
        bias[...] = jnp.where(same & (along < cells_here), 0.0, MASKED)
    masks = head_masks()
    u = cells[:, :width]
    target = cells[:, width : width + 3]
    tok_ref[0] = u.astype(BF16)
    mean_row = jnp.mean(u, axis=-1, keepdims=True)
    centred = u - mean_row
    variance = jnp.mean(centred * centred, axis=-1, keepdims=True)
    normed = (centred * lax.rsqrt(variance + EPSILON)).astype(BF16)
    qkv_s[...] = mm(normed, wqkv_ref[...]).astype(BF16)

    def forward(g, _):
        at = pl.multiple_of(g * GROUP, GROUP)
        for b, (start, rows, _) in enumerate(BLOCKS):
            span = pl.ds(start, rows)
            q = qkv_s[span, pl.ds(at, GROUP)]
            k = qkv_s[span, pl.ds(inner + at, GROUP)]
            v = qkv_s[span, pl.ds(2 * inner + at, GROUP)]
            heads = range(PER_GROUP)
            scores = [mm_nt(q * masks[h], k) + bias_refs[b][...] for h in heads]
            tops = [jnp.max(s, axis=-1, keepdims=True) for s in scores]
            exps = [
                jnp.exp2((s - top) * (scale * 1.4426950408889634)) for s, top in zip(scores, tops)
            ]
            probs = [e * (1.0 / jnp.sum(e, axis=-1, keepdims=True)) for e in exps]
            for h in heads:
                p_refs[b][g * PER_GROUP + h] = probs[h]
            total = sum(mm(probs[h].astype(BF16), v * masks[h]) for h in heads)
            mixed_s[span, pl.ds(at, GROUP)] = total.astype(BF16)
        return 0

    lax.fori_loop(0, groups, forward, 0)

    mixed = mixed_s[...]
    output = u + mm(mixed, proj_ref[...])
    logits = mm_nt(output.astype(BF16), headt_ref[...])
    row = lax.broadcasted_iota(jnp.int32, (ROWS, 1), 0)
    real = (row < LOW_CELLS) | ((row >= LOW_ROWS) & (row < LOW_ROWS + HIGH_CELLS))
    logit_grad = LOSS_SCALE * (jax.nn.sigmoid(logits) - target)
    logit_grad = jnp.where(real, logit_grad, 0.0)
    lg_ref[0] = logit_grad
    grad_low = output_grad_of(logit_grad, headt_ref).astype(BF16)
    mg_s[...] = mm_nt(grad_low, proj_ref[...]).astype(BF16)
    for start, rows, _ in BLOCKS:
        acc_p[...] += mm(grad_low[start : start + rows].T, mixed[start : start + rows])

    def backward(g, _):
        at = pl.multiple_of(g * GROUP, GROUP)
        sets = []
        for b, (start, rows, _) in enumerate(BLOCKS):
            span = pl.ds(start, rows)
            q = qkv_s[span, pl.ds(at, GROUP)]
            k = qkv_s[span, pl.ds(inner + at, GROUP)]
            v = qkv_s[span, pl.ds(2 * inner + at, GROUP)]
            mg = mg_s[span, pl.ds(at, GROUP)]
            q_t = q.T
            mg_t = mg.T
            sets.append((b, span, q, k, v.T, mg, q_t, mg_t))
        heads = range(PER_GROUP)
        grads = [[mm(t[5] * masks[h], t[4]) for h in heads] for t in sets]
        all_values = [
            [
                mm(t[7][h * HEAD : (h + 1) * HEAD], p_refs[t[0]][g * PER_GROUP + h].astype(BF16))
                for h in heads
            ]
            for t in sets
        ]
        for t, grad, value_parts in zip(sets, grads, all_values):
            b, span, q, k, _, mg, q_t, mg_t = t
            ps = [p_refs[b][g * PER_GROUP + h] for h in heads]
            alongs = [jnp.sum(grad[h] * ps[h], axis=-1, keepdims=True) for h in heads]
            lows = [(ps[h] * (grad[h] - alongs[h]) * scale).astype(BF16) for h in heads]
            query_grad = sum(mm(lows[h], k * masks[h]) for h in heads)
            key_parts = [mm(q_t[h * HEAD : (h + 1) * HEAD], lows[h]) for h in heads]
            d_ref[0, span, pl.ds(at, GROUP)] = query_grad.astype(BF16)
            key_t = jnp.concatenate(key_parts, axis=0).astype(BF16)
            value_t = jnp.concatenate(value_parts, axis=0).astype(BF16)
            d_ref[0, span, pl.ds(inner + at, GROUP)] = key_t.T
            d_ref[0, span, pl.ds(2 * inner + at, GROUP)] = value_t.T
        return 0

    lax.fori_loop(0, groups, backward, 0)

    for start, rows, _ in BLOCKS:
        span = slice(start, start + rows)
        acc_q[...] += mm(normed[span].T, d_ref[0, span, :])


def output_grad_of(logit_grad, headt_ref):
    head = headt_ref[...].astype(F32)
    return (
        logit_grad[:, 0:1] * head[0:1]
        + logit_grad[:, 1:2] * head[1:2]
        + logit_grad[:, 2:3] * head[2:3]
    )


def first_kernel(info, vol_ref, aff_ref, index_ref, *rest):
    weights, outs, acc_q, acc_p = rest[:3], rest[3:6], rest[6], rest[7]
    own, scratch = rest[8], rest[9:]
    acc_q[...] = jnp.zeros_like(acc_q)
    acc_p[...] = jnp.zeros_like(acc_p)

    @pl.when(info[0] != 0)
    def _():
        own[...] = jnp.zeros_like(own)
        xs = ys = list(range(MARGIN, MARGIN + WIN))
        sources = take_own(vol_ref, aff_ref, own, xs, ys)
        sources = jnp.concatenate([sources, jnp.zeros((8, sources.shape[1]), BF16)], axis=0)
        cells = gather_rows(index_ref[0], sources)
        window_terms(info, 0, cells, weights, outs, acc_q, acc_p, scratch)


def rest_kernel(info, vol_ref, aff_ref, side_ref, front_ref, corner_ref, index_ref, *rest):
    weights, in_q, in_p = rest[:3], rest[3], rest[4]
    outs, keep_ref, send_ref = rest[8:11], rest[11], rest[12]
    acc_q, acc_p, first_q, first_p, sems, cells, own = rest[13:20]
    scratch = rest[20:]
    loads = (
        pltpu.make_async_copy(in_q, first_q, sems.at[0]),
        pltpu.make_async_copy(in_p, first_p, sems.at[1]),
    )
    window = pl.program_id(0) + 1
    near = list(range(MARGIN, MARGIN + WIN))
    far = list(range(MARGIN + WIN, 2 * WIN))

    @pl.when(window == 1)
    def _():
        for load in loads:
            load.start()
        acc_q[...] = jnp.zeros_like(acc_q)
        acc_p[...] = jnp.zeros_like(acc_p)
        own[...] = jnp.zeros_like(own)

    @pl.when((window == 1) & (info[1] != 0))
    def _():
        sources = jnp.concatenate(
            [take_own(vol_ref, aff_ref, own, near, far), side_ref[0:160]], axis=0
        )
        cells[...] = gather_rows(index_ref[0], sources)

    @pl.when((window == 2) & (info[2] != 0))
    def _():
        sources = jnp.concatenate(
            [take_own(vol_ref, aff_ref, own, far, near), front_ref[0:208]], axis=0
        )
        cells[...] = gather_rows(index_ref[0], sources)

    @pl.when((window == 3) & (info[3] != 0))
    def _():
        sources = jnp.concatenate(
            [
                take_own(vol_ref, aff_ref, own, far, far),
                side_ref[144:240],
                front_ref[48:240],
                corner_ref[...],
            ],
            axis=0,
        )
        cells[...] = gather_rows(index_ref[0], sources)

    @pl.when(info[window] != 0)
    def _():
        window_terms(info, window, cells[...], weights, outs, acc_q, acc_p, scratch)

    @pl.when(window == 3)
    def _():
        inner = acc_p.shape[1]
        share = acc_p.shape[0] // 16
        core = info[6]
        for load in loads:
            load.wait()

        def one(i, _):
            mine = pl.ds(pl.multiple_of((i * 2 + core) * share, 16), share)
            other = pl.ds(pl.multiple_of((i * 2 + 1 - core) * share, 16), share)
            y, near = lax.div(i, 2), lax.rem(i, 2)
            for part in range(3):
                at = slice(part * inner, (part + 1) * inner)
                keep_ref[y, part, near] = acc_q[mine, at] + first_q[mine, at]
                send_ref[y, part, near] = (acc_q[other, at] + first_q[other, at]).astype(BF16)
            keep_ref[y, 3, near] = acc_p[mine, :] + first_p[mine, :]
            send_ref[y, 3, near] = (acc_p[other, :] + first_p[other, :]).astype(BF16)
            return 0

        lax.fori_loop(0, 8, one, 0)


def window_pieces(window):
    a, b = window // 2, window % 2
    x_near = OUTER if a else WIN
    y_near = OUTER if b else WIN
    x_at, y_at = MARGIN + a * WIN, MARGIN + b * WIN
    pieces = [(0, 0, x_near, 0, y_near, x_at, y_at)]
    if b:
        pieces.append((1, 0, x_near, y_near, WIN, a * WIN, 0))
    if a:
        pieces.append((2, x_near, WIN, 0, y_near, 0, b * WIN))
    if a and b:
        pieces.append((3, x_near, WIN, y_near, WIN, 0, 0))
    return pieces


def cell_kernel(windows, held, info, tok_ref, lg_ref, d_ref, wqkv_ref, headt_ref, index_ref, *rest):
    *targets, cell, sems = rest[held:]
    if held:
        targets = {0: targets[0], 2: targets[1]}
    step = pl.program_id(0)
    window = jnp.where(step == 0, windows[0], windows[1])

    @pl.when(info[window] == 0)
    def _():
        cell[step] = jnp.zeros_like(cell[step])

    @pl.when(info[window] != 0)
    def _():
        u = tok_ref[0].astype(F32)
        mean_row = jnp.mean(u, axis=-1, keepdims=True)
        centred = u - mean_row
        variance = jnp.mean(centred * centred, axis=-1, keepdims=True)
        inv_std = lax.rsqrt(variance + EPSILON)
        unit_rows = centred * inv_std
        normed_grad = mm_nt(d_ref[0], wqkv_ref[...])
        grad_mean = jnp.mean(normed_grad, axis=-1, keepdims=True)
        grad_along = jnp.mean(normed_grad * unit_rows, axis=-1, keepdims=True)
        output_grad = output_grad_of(lg_ref[0], headt_ref)
        cell_low = output_grad + inv_std * (normed_grad - grad_mean - unit_rows * grad_along)
        at = lax.broadcasted_iota(jnp.int32, (WIN * WIN * 8, ROWS), 0)
        chosen = jnp.where(index_ref[0:1, :] == at, 1.0, 0.0).astype(BF16)
        placed = mm(chosen, cell_low.astype(BF16))
        placed = placed.reshape(WIN * WIN, 8, placed.shape[1])[:, :WIN].astype(BF16)
        cell[step] = placed.reshape(WIN, WIN, WIN, placed.shape[2])

    def copies(j):
        made = []
        for n, (t, x0, x1, y0, y1, to_x, to_y) in enumerate(window_pieces(windows[j])):
            made.append(
                pltpu.make_async_copy(
                    cell.at[j, x0:x1, y0:y1],
                    targets[t].at[to_x : to_x + x1 - x0, to_y : to_y + y1 - y0],
                    sems.at[j, n],
                )
            )
        return made

    @pl.when(step == 0)
    def _():
        for copy in copies(0):
            copy.start()

    @pl.when(step == 1)
    def _():
        for copy in copies(1):
            copy.start()
        for copy in copies(0) + copies(1):
            copy.wait()


def whole(shape):
    return pl.BlockSpec(shape, lambda i, *_: (0,) * len(shape))


def by_window(shape, first):
    return pl.BlockSpec((1,) + shape, lambda i, *_: (i + first,) + (0,) * len(shape))


PARAMS = pltpu.CompilerParams(vmem_limit_bytes=56 * 1024 * 1024)


def kept_shapes(width, inner):
    return [((ROWS, width), BF16), ((ROWS, 3), F32), ((ROWS, 3 * inner), BF16)]


def work_shapes(inner, width):
    heads = inner // HEAD
    return [
        pltpu.VMEM((64, 8, width + GROUP), F32),
        pltpu.VMEM((ROWS, 3 * inner), BF16),
        pltpu.VMEM((ROWS, inner), BF16),
        pltpu.VMEM((ROWS, inner), BF16),
        pltpu.VMEM((heads, LOW_ROWS, LOW_ROWS), F32),
        pltpu.VMEM((heads, HIGH_ROWS, HIGH_ROWS), F32),
        pltpu.VMEM((LOW_ROWS, LOW_ROWS), F32),
        pltpu.VMEM((HIGH_ROWS, HIGH_ROWS), F32),
    ]


def run_first(info, vol, aff, weights):
    inner, width = weights[1].shape
    kept = kept_shapes(width, inner)
    terms = [(width, 3 * inner), (width, inner)]
    return pl.pallas_call(
        first_kernel,
        name="first_window",
        grid_spec=pltpu.PrefetchScalarGridSpec(
            num_scalar_prefetch=1,
            grid=(1,),
            in_specs=[
                whole(vol.shape),
                whole(aff.shape),
                pl.BlockSpec((1, 8, 3 * GROUP), lambda i, *_: (0, 0, 0)),
                *[whole(w.shape) for w in weights],
            ],
            out_specs=[by_window(s, 0) for s, _ in kept] + [whole(s) for s in terms],
            scratch_shapes=work_shapes(inner, width),
        ),
        out_shape=[jax.ShapeDtypeStruct((4,) + s, d) for s, d in kept]
        + [jax.ShapeDtypeStruct(s, F32) for s in terms],
        compiler_params=PARAMS,
    )(info, vol, aff, jnp.asarray(source_rows()), *weights)


def run_rest(info, vol, aff, rims, weights, terms, kept_values):
    inner, width = weights[1].shape
    share = width // 16
    kept = kept_shapes(width, inner)
    return pl.pallas_call(
        rest_kernel,
        name="rest_windows",
        grid_spec=pltpu.PrefetchScalarGridSpec(
            num_scalar_prefetch=1,
            grid=(3,),
            in_specs=[
                whole(vol.shape),
                whole(aff.shape),
                *[whole(r.shape) for r in rims],
                pl.BlockSpec((1, 8, 3 * GROUP), lambda i, *_: (i + 1, 0, 0)),
                *[whole(w.shape) for w in weights],
                *[pl.BlockSpec(memory_space=pl.ANY) for _ in (*terms, *kept)],
            ],
            out_specs=[by_window(s, 1) for s, _ in kept] + [whole((4, 4, 2, share, inner))] * 2,
            scratch_shapes=[
                *[pltpu.VMEM((width, n * inner), F32) for n in (3, 1, 3, 1)],
                pltpu.SemaphoreType.DMA((2,)),
                pltpu.VMEM((ROWS, width + GROUP), F32),
            ]
            + work_shapes(inner, width),
        ),
        out_shape=[jax.ShapeDtypeStruct((4,) + s, d) for s, d in kept]
        + [
            jax.ShapeDtypeStruct((4, 4, 2, share, inner), F32),
            jax.ShapeDtypeStruct((4, 4, 2, share, inner), BF16),
        ],
        input_output_aliases={12 + i: i for i in range(3)},
        compiler_params=PARAMS,
    )(info, vol, aff, *rims, jnp.asarray(source_rows()), *weights, *terms, *kept_values)


def run_cells(windows, info, kept, wqkv, head_t, size_x, size_y, held):
    width = kept[0].shape[2]
    rest_x, rest_y = size_x - MARGIN, size_y - MARGIN
    first, change = windows[0], windows[1] - windows[0]

    def turned(shape):
        return pl.BlockSpec(
            (1,) + shape, lambda i, *_: (first + change * i,) + (0,) * len(shape)
        )

    shapes = [
        (size_x, size_y, WIN, width),
        (rest_x, MARGIN, WIN, width),
        (MARGIN, rest_y, WIN, width),
        (MARGIN, MARGIN, WIN, width),
    ]
    if held:
        shapes = [h.shape for h in held]
    anywhere = pl.BlockSpec(memory_space=pl.ANY)
    kernel = functools.partial(cell_kernel, windows, len(held))
    return pl.pallas_call(
        kernel,
        name="cell_grads",
        grid_spec=pltpu.PrefetchScalarGridSpec(
            num_scalar_prefetch=1,
            grid=(2,),
            in_specs=[
                *[turned(k.shape[1:]) for k in kept],
                whole(wqkv.shape),
                whole(head_t.shape),
                whole((8, ROWS)),
                *[anywhere for _ in held],
            ],
            out_specs=[anywhere] * len(shapes),
            scratch_shapes=[
                pltpu.VMEM((2, WIN, WIN, WIN, width), BF16),
                pltpu.SemaphoreType.DMA((2, 4)),
            ],
        ),
        out_shape=[jax.ShapeDtypeStruct(s, BF16) for s in shapes],
        input_output_aliases={7 + i: i for i in range(len(held))},
        compiler_params=PARAMS,
    )(info, *kept, wqkv, head_t, jnp.asarray(grid_rows()), *held)


def shifted(block, axes, shifts, sizes):
    first, second = sizes
    route = []
    for i in range(first):
        for j in range(second):
            to = ((i + shifts[0]) % first) * second + (j + shifts[1]) % second
            route.append((i * second + j, to))
    return lax.ppermute(block, axes, route)


def rim_message(vol, aff, rows):
    flat = jnp.concatenate([vol, aff], axis=-1)
    flat = flat.reshape(-1, flat.shape[-1])
    return jnp.pad(flat, ((0, rows - flat.shape[0]), (0, 0)))


def outgoing(total, position):
    size = total.shape[0]
    parts = []
    for shift in range(1, size):
        to = lax.rem(position + shift, size)
        parts.append(lax.dynamic_index_in_dim(total, to, 0, keepdims=False).astype(BF16))
    return parts


def incoming(total, position, got):
    mine = lax.dynamic_index_in_dim(total, position, 0, keepdims=False)
    for part in got:
        mine = mine + part.astype(F32)
    return mine


def axis_shares(total, axis, position):
    size = total.shape[0]
    got = [
        lax.ppermute(part, axis, [(i, (i + shift + 1) % size) for i in range(size)])
        for shift, part in enumerate(outgoing(total, position))
    ]
    return incoming(total, position, got)


def exchanged(parts, routes):
    return [lax.ppermute(part, "ga", route) for part, route in zip(parts, routes)]


def gathered(part, position, size):
    result = jnp.zeros((size,) + part.shape, part.dtype)
    result = lax.dynamic_update_index_in_dim(result, part, position, 0)
    for shift in range(1, size):
        got = lax.ppermute(part, "gy", [(i, (i + shift) % size) for i in range(size)])
        source = lax.rem(position + size - shift, size)
        result = lax.dynamic_update_index_in_dim(result, got, source, 0)
    return result


def per_device(volume, affinity, window_dest, qkv_weight, proj_weight, head_weight):
    size_x, size_y = volume.shape[1], volume.shape[2]
    n_gy, n_gx, n_ga = lax.axis_size("gy"), lax.axis_size("gx"), lax.axis_size("ga")
    gy, gx, ga = lax.axis_index("gy"), lax.axis_index("gx"), lax.axis_index("ga")
    m = MARGIN
    vol = volume[0]
    aff = jnp.pad(affinity[0].transpose(1, 2, 3, 0), ((0, 0), (0, 0), (0, 0), (0, GROUP - 3)))
    sizes = (n_gy, n_gx)
    axes = ("gy", "gx")

    side = shifted(rim_message(vol[m:, :m], aff[m:, :m], RIM_ROWS), axes, (0, -1), sizes)
    front = shifted(rim_message(vol[:m, m:], aff[:m, m:], RIM_ROWS), axes, (-1, 0), sizes)
    corner = shifted(rim_message(vol[:m, :m], aff[:m, :m], CORNER_ROWS), axes, (-1, -1), sizes)

    slot = lax.iota(jnp.int32, 8)
    live = jnp.pad(window_dest.reshape(-1), (0, 4))
    info = jnp.where(slot < 4, live < n_ga, False)
    info = info | ((slot == 4) & (gy == n_gy - 1)) | ((slot == 5) & (gx == n_gx - 1))
    info = (info | ((slot >= 6) & (lax.rem(ga, 2) == 1))).astype(jnp.int32)
    head_t = head_weight.T
    weights = (qkv_weight, proj_weight, head_t)

    *kept, term_q, term_p = run_first(info, vol, aff, weights)
    *kept, keep, send = run_rest(
        info, vol, aff, (side, front, corner), weights, (term_q, term_p), kept
    )
    info, send = lax.optimization_barrier((info, send))
    (got,) = exchanged([send], [[(i, i ^ 1) for i in range(n_ga)]])
    main, back_side, back_front, back_corner = run_cells(
        (3, 1), info, kept, qkv_weight, head_t, size_x, size_y, ()
    )
    total = keep + got.astype(F32)
    along = lax.div(ga, 4)
    parts = outgoing(total, along)
    info, back_side, back_corner, parts = lax.optimization_barrier(
        (info, back_side, back_corner, parts)
    )
    got = exchanged(
        parts, [[(i, (i + 4 * s) % n_ga) for i in range(n_ga)] for s in range(1, 4)]
    )
    back_side = shifted(back_side, axes, (0, 1), sizes)
    main, back_front = run_cells(
        (2, 0), info, kept, qkv_weight, head_t, size_x, size_y, (main, back_front)
    )
    total, back_front = lax.optimization_barrier((total, back_front))
    total = incoming(total, along, got)
    total = axis_shares(total, "gy", gy)
    total, back_side = lax.optimization_barrier((total, back_side))
    near = lax.rem(lax.div(ga, 2), 2)
    parts = outgoing(total, near)
    got = exchanged(parts, [[(i, i ^ 2) for i in range(n_ga)]])
    back_front = shifted(back_front, axes, (1, 0), sizes)
    back_corner = shifted(back_corner, axes, (1, 1), sizes)
    total = incoming(total, near, got)
    low = total.astype(BF16)
    for shift in range(1, n_gx):
        route = [(i, (i + shift) % n_gx) for i in range(n_gx)]
        total = total + lax.ppermute(low, "gx", route).astype(F32)
    total, back_front, back_corner = lax.optimization_barrier((total, back_front, back_corner))
    main = lax.dynamic_update_slice(main, back_side, (m, 0, 0, 0))
    main = lax.dynamic_update_slice(main, back_front, (0, m, 0, 0))
    main = lax.dynamic_update_slice(main, back_corner, (0, 0, 0, 0))
    total = total * (float(n_gy * n_gx * n_ga * 2 * WIN**3) ** (-0.5))
    parts = gathered(total, gy, n_gy)
    grad_qkv = jnp.concatenate([parts[0], parts[1], parts[2]], axis=1)
    return (main[None], grad_qkv, parts[3].T)


def solution(mesh):
    placed = (
        P("ga", "gy", "gx", None, None),
        P("ga", None, "gy", "gx", None),
        P("ga", "gy", "gx", None),
        P(),
        P(),
        P(),
    )
    return jax.shard_map(
        per_device,
        mesh=mesh,
        in_specs=placed,
        out_specs=(P("ga", "gy", "gx", None, None), P("ga", None), P(None, "ga")),
        check_vma=False,
    )
```

```python
import functools

import jax
import jax.numpy as jnp
import numpy as np
from jax import lax
from jax.experimental import pallas as pl
from jax.experimental.pallas import tpu as pltpu
from jax.sharding import PartitionSpec as P


HEAD = 32
WIN = 7
MARGIN = 3
LOSS_SCALE = 32.0
EPSILON = 1e-05
LOW_CELLS = 147
HIGH_CELLS = 196
LOW_ROWS = 160
HIGH_ROWS = 208
ROWS = LOW_ROWS + HIGH_ROWS
BLOCKS = ((0, LOW_ROWS, LOW_CELLS), (LOW_ROWS, HIGH_ROWS, HIGH_CELLS))
GROUP = 128
PER_GROUP = GROUP // HEAD
MASKED = -1e30
RIM_ROWS = 240
CORNER_ROWS = 64
LOW_Z = 3
OUTER = 4
F32 = jnp.float32
BF16 = jnp.bfloat16


def mm(a, b):
    return lax.dot_general(a, b, (((1,), (0,)), ((), ())), preferred_element_type=F32)


def mm_nt(a, b):
    return lax.dot_general(a, b, (((1,), (1,)), ((), ())), preferred_element_type=F32)


def row_cells():
    cells = np.full((ROWS, 3), -1)
    for z in range(WIN):
        for x in range(WIN):
            for y in range(WIN):
                if z < LOW_Z:
                    row = z * 49 + x * WIN + y
                else:
                    row = LOW_ROWS + (z - LOW_Z) * 49 + x * WIN + y
                cells[row] = (x, y, z)
    return cells


def source_rows():
    rest = 2 * WIN - MARGIN
    table = np.full((4, ROWS), -1)
    for row, (x, y, z) in enumerate(row_cells()):
        if x < 0:
            continue
        table[0, row] = (x * WIN + y) * 8 + z
        if y < OUTER:
            table[1, row] = (x * OUTER + y) * 8 + z
        else:
            table[1, row] = 224 + (x * MARGIN + y - OUTER) * WIN + z
        if x < OUTER:
            table[2, row] = (x * WIN + y) * 8 + z
        else:
            table[2, row] = 224 + ((x - OUTER) * rest + y) * WIN + z
        if x < OUTER and y < OUTER:
            table[3, row] = (x * OUTER + y) * 8 + z
        elif x < OUTER:
            table[3, row] = 128 + ((x + WIN) * MARGIN + y - OUTER) * WIN + z - 144
        elif y < OUTER:
            table[3, row] = 224 + ((x - OUTER) * rest + y + WIN) * WIN + z - 48
        else:
            table[3, row] = 416 + ((x - OUTER) * MARGIN + y - OUTER) * WIN + z
    table = np.pad(table, ((0, 0), (0, 3 * GROUP - ROWS)), constant_values=-1)
    return np.repeat(table[:, None, :], 8, axis=1).astype(np.float32)


def grid_rows():
    table = np.full((8, ROWS), -1)
    for row, (x, y, z) in enumerate(row_cells()):
        if x >= 0:
            table[:, row] = (x * WIN + y) * 8 + z
    return table.astype(np.int32)


def edge_code(index, edge_x, edge_y):
    by_row = jnp.floor((index + 0.5) * (1.0 / 7.0))
    y = index - 7.0 * by_row
    z = jnp.floor((by_row + 0.5) * (1.0 / 7.0))
    x = by_row - 7.0 * z
    on_x = jnp.where(x >= 4.0, edge_x, 0.0)
    on_y = jnp.where(y >= 4.0, edge_y, 0.0)
    return 2.0 * on_x + on_y


def head_masks():
    lane = lax.broadcasted_iota(jnp.int32, (1, GROUP), 1)
    return [
        jnp.where((lane >= h * HEAD) & (lane < (h + 1) * HEAD), 1.0, 0.0).astype(BF16)
        for h in range(PER_GROUP)
    ]


def take_own(vol_ref, aff_ref, own, xs, ys):
    count = len(xs) * len(ys)
    width = vol_ref.shape[-1]
    for i, x in enumerate(xs):
        at = slice(i * len(ys), (i + 1) * len(ys))
        own[at, 0:WIN, 0:width] = vol_ref[x, ys[0] : ys[-1] + 1].astype(F32)
        own[at, 0:WIN, width:] = aff_ref[x, ys[0] : ys[-1] + 1].astype(F32)
    rows = count * 8
    return own[0:count].reshape(rows, own.shape[-1]).astype(BF16)


def gather_rows(index, sources):
    depth = sources.shape[0]
    at = lax.broadcasted_iota(jnp.int32, (ROWS, depth), 1)
    column = index.T[:ROWS, 0:1].astype(jnp.int32)
    chosen = jnp.where(column == at, 1.0, 0.0).astype(BF16)
    return mm(chosen, sources)


def window_terms(info, window, cells, weights, outs, acc_q, acc_p, scratch, fresh):
    wqkv_ref, proj_ref, headt_ref = weights
    tok_ref, lg_ref, d_ref = outs
    qkv_s, mixed_s, mg_s, p_low, p_high, bias_low, bias_high = scratch
    inner, width = proj_ref.shape
    groups = inner // GROUP
    scale = HEAD ** (-0.5)
    p_refs = (p_low, p_high)
    bias_refs = (bias_low, bias_high)
    edge_x = jnp.where((info[4] != 0) & (window >= 2), 1.0, 0.0)
    edge_y = jnp.where((info[5] != 0) & (lax.rem(window, 2) == 1), 1.0, 0.0)
    for (_, rows, cells_here), bias in zip(BLOCKS, bias_refs):
        down = lax.broadcasted_iota(jnp.int32, (rows, 1), 0).astype(F32)
        along = lax.broadcasted_iota(jnp.int32, (1, rows), 1).astype(F32)
        same = edge_code(down, edge_x, edge_y) == edge_code(along, edge_x, edge_y)
        bias[...] = jnp.where(same & (along < cells_here), 0.0, MASKED)
    masks = head_masks()
    u = cells[:, :width]
    target = cells[:, width : width + 3]
    tok_ref[0] = u.astype(BF16)
    mean_row = jnp.mean(u, axis=-1, keepdims=True)
    centred = u - mean_row
    variance = jnp.mean(centred * centred, axis=-1, keepdims=True)
    normed = (centred * lax.rsqrt(variance + EPSILON)).astype(BF16)
    qkv_s[...] = mm(normed, wqkv_ref[...]).astype(BF16)

    def forward(g, _):
        at = pl.multiple_of(g * GROUP, GROUP)
        for b, (start, rows, _) in enumerate(BLOCKS):
            span = pl.ds(start, rows)
            q = qkv_s[span, pl.ds(at, GROUP)]
            k = qkv_s[span, pl.ds(inner + at, GROUP)]
            v = qkv_s[span, pl.ds(2 * inner + at, GROUP)]
            heads = range(PER_GROUP)
            scores = [mm_nt(q * masks[h], k) + bias_refs[b][...] for h in heads]
            tops = [jnp.max(s, axis=-1, keepdims=True) for s in scores]
            exps = [
                jnp.exp2((s - top) * (scale * 1.4426950408889634)) for s, top in zip(scores, tops)
            ]
            probs = [e * (1.0 / jnp.sum(e, axis=-1, keepdims=True)) for e in exps]
            for h in heads:
                p_refs[b][g * PER_GROUP + h] = probs[h]
            total = sum(mm(probs[h].astype(BF16), v * masks[h]) for h in heads)
            mixed_s[span, pl.ds(at, GROUP)] = total.astype(BF16)
        return 0

    lax.fori_loop(0, groups, forward, 0)

    mixed = mixed_s[...]
    output = u + mm(mixed, proj_ref[...])
    logits = mm_nt(output.astype(BF16), headt_ref[...])
    row = lax.broadcasted_iota(jnp.int32, (ROWS, 1), 0)
    real = (row < LOW_CELLS) | ((row >= LOW_ROWS) & (row < LOW_ROWS + HIGH_CELLS))
    logit_grad = LOSS_SCALE * (jax.nn.sigmoid(logits) - target)
    logit_grad = jnp.where(real, logit_grad, 0.0)
    lg_ref[0] = logit_grad
    grad_low = output_grad_of(logit_grad, headt_ref).astype(BF16)
    mg_s[...] = mm_nt(grad_low, proj_ref[...]).astype(BF16)
    for start, rows, _ in BLOCKS:
        term = mm(grad_low[start : start + rows].T, mixed[start : start + rows])
        acc_p[...] = term if fresh and start == 0 else acc_p[...] + term

    def backward(g, _):
        at = pl.multiple_of(g * GROUP, GROUP)
        sets = []
        for b, (start, rows, _) in enumerate(BLOCKS):
            span = pl.ds(start, rows)
            q = qkv_s[span, pl.ds(at, GROUP)]
            k = qkv_s[span, pl.ds(inner + at, GROUP)]
            v = qkv_s[span, pl.ds(2 * inner + at, GROUP)]
            mg = mg_s[span, pl.ds(at, GROUP)]
            q_t = q.T
            mg_t = mg.T
            sets.append((b, span, q, k, v.T, mg, q_t, mg_t))
        heads = range(PER_GROUP)
        grads = [[mm(t[5] * masks[h], t[4]) for h in heads] for t in sets]
        all_values = [
            [
                mm(t[7][h * HEAD : (h + 1) * HEAD], p_refs[t[0]][g * PER_GROUP + h].astype(BF16))
                for h in heads
            ]
            for t in sets
        ]
        for t, grad, value_parts in zip(sets, grads, all_values):
            b, span, q, k, _, mg, q_t, mg_t = t
            ps = [p_refs[b][g * PER_GROUP + h] for h in heads]
            alongs = [jnp.sum(grad[h] * ps[h], axis=-1, keepdims=True) for h in heads]
            lows = [(ps[h] * (grad[h] - alongs[h]) * scale).astype(BF16) for h in heads]
            query_grad = sum(mm(lows[h], k * masks[h]) for h in heads)
            key_parts = [mm(q_t[h * HEAD : (h + 1) * HEAD], lows[h]) for h in heads]
            d_ref[0, span, pl.ds(at, GROUP)] = query_grad.astype(BF16)
            key_t = jnp.concatenate(key_parts, axis=0).astype(BF16)
            value_t = jnp.concatenate(value_parts, axis=0).astype(BF16)
            d_ref[0, span, pl.ds(inner + at, GROUP)] = key_t.T
            d_ref[0, span, pl.ds(2 * inner + at, GROUP)] = value_t.T
        return 0

    lax.fori_loop(0, groups, backward, 0)

    for start, rows, _ in BLOCKS:
        span = slice(start, start + rows)
        term = mm(normed[span].T, d_ref[0, span, :])
        acc_q[...] = term if fresh and start == 0 else acc_q[...] + term


def output_grad_of(logit_grad, headt_ref):
    head = headt_ref[...].astype(F32)
    return (
        logit_grad[:, 0:1] * head[0:1]
        + logit_grad[:, 1:2] * head[1:2]
        + logit_grad[:, 2:3] * head[2:3]
    )


def first_kernel(info, vol_ref, aff_ref, index_ref, *rest):
    weights, outs, acc_q, acc_p = rest[:3], rest[3:6], rest[6], rest[7]
    own, scratch = rest[8], rest[9:]

    @pl.when(info[0] == 0)
    def _():
        acc_q[...] = jnp.zeros_like(acc_q)
        acc_p[...] = jnp.zeros_like(acc_p)

    @pl.when(info[0] != 0)
    def _():
        own[...] = jnp.zeros_like(own)
        xs = ys = list(range(MARGIN, MARGIN + WIN))
        sources = take_own(vol_ref, aff_ref, own, xs, ys)
        sources = jnp.concatenate([sources, jnp.zeros((8, sources.shape[1]), BF16)], axis=0)
        cells = gather_rows(index_ref[0], sources)
        window_terms(info, 0, cells, weights, outs, acc_q, acc_p, scratch, True)


def rest_kernel(info, vol_ref, aff_ref, side_ref, front_ref, corner_ref, index_ref, *rest):
    weights, in_q, in_p = rest[:3], rest[3], rest[4]
    outs, keep_ref, send_ref = rest[8:11], rest[11], rest[12]
    acc_q, acc_p, first_q, first_p, sems, cells, own = rest[13:20]
    scratch = rest[20:]
    loads = (
        pltpu.make_async_copy(in_q, first_q, sems.at[0]),
        pltpu.make_async_copy(in_p, first_p, sems.at[1]),
    )
    window = pl.program_id(0) + 1
    near = list(range(MARGIN, MARGIN + WIN))
    far = list(range(MARGIN + WIN, 2 * WIN))

    @pl.when(window == 1)
    def _():
        for load in loads:
            load.start()
        acc_q[...] = jnp.zeros_like(acc_q)
        acc_p[...] = jnp.zeros_like(acc_p)
        own[...] = jnp.zeros_like(own)

    @pl.when((window == 1) & (info[1] != 0))
    def _():
        sources = jnp.concatenate(
            [take_own(vol_ref, aff_ref, own, near, far), side_ref[0:160]], axis=0
        )
        cells[...] = gather_rows(index_ref[0], sources)

    @pl.when((window == 2) & (info[2] != 0))
    def _():
        sources = jnp.concatenate(
            [take_own(vol_ref, aff_ref, own, far, near), front_ref[0:208]], axis=0
        )
        cells[...] = gather_rows(index_ref[0], sources)

    @pl.when((window == 3) & (info[3] != 0))
    def _():
        sources = jnp.concatenate(
            [
                take_own(vol_ref, aff_ref, own, far, far),
                side_ref[144:240],
                front_ref[48:240],
                corner_ref[...],
            ],
            axis=0,
        )
        cells[...] = gather_rows(index_ref[0], sources)

    @pl.when(info[window] != 0)
    def _():
        window_terms(info, window, cells[...], weights, outs, acc_q, acc_p, scratch, False)

    @pl.when(window == 3)
    def _():
        inner = acc_p.shape[1]
        share = acc_p.shape[0] // 16
        core = info[6]
        for load in loads:
            load.wait()

        def one(i, _):
            mine = pl.ds(pl.multiple_of((i * 2 + core) * share, 16), share)
            other = pl.ds(pl.multiple_of((i * 2 + 1 - core) * share, 16), share)
            y, near = lax.div(i, 2), lax.rem(i, 2)
            for part in range(3):
                at = slice(part * inner, (part + 1) * inner)
                keep_ref[y, part, near] = acc_q[mine, at] + first_q[mine, at]
                send_ref[y, part, near] = (acc_q[other, at] + first_q[other, at]).astype(BF16)
            keep_ref[y, 3, near] = acc_p[mine, :] + first_p[mine, :]
            send_ref[y, 3, near] = (acc_p[other, :] + first_p[other, :]).astype(BF16)
            return 0

        lax.fori_loop(0, 8, one, 0)


def window_pieces(window):
    a, b = window // 2, window % 2
    x_near = OUTER if a else WIN
    y_near = OUTER if b else WIN
    x_at, y_at = MARGIN + a * WIN, MARGIN + b * WIN
    pieces = [(0, 0, x_near, 0, y_near, x_at, y_at)]
    if b:
        pieces.append((1, 0, x_near, y_near, WIN, a * WIN, 0))
    if a:
        pieces.append((2, x_near, WIN, 0, y_near, 0, b * WIN))
    if a and b:
        pieces.append((3, x_near, WIN, y_near, WIN, 0, 0))
    return pieces


def cell_kernel(windows, held, info, tok_ref, lg_ref, d_ref, wqkv_ref, headt_ref, index_ref, *rest):
    *targets, cell, sems = rest[held:]
    if held:
        targets = {0: targets[0], 2: targets[1]}
    step = pl.program_id(0)
    window = jnp.where(step == 0, windows[0], windows[1])

    @pl.when(info[window] == 0)
    def _():
        cell[step] = jnp.zeros_like(cell[step])

    @pl.when(info[window] != 0)
    def _():
        u = tok_ref[0].astype(F32)
        mean_row = jnp.mean(u, axis=-1, keepdims=True)
        centred = u - mean_row
        variance = jnp.mean(centred * centred, axis=-1, keepdims=True)
        inv_std = lax.rsqrt(variance + EPSILON)
        unit_rows = centred * inv_std
        normed_grad = mm_nt(d_ref[0], wqkv_ref[...])
        grad_mean = jnp.mean(normed_grad, axis=-1, keepdims=True)
        grad_along = jnp.mean(normed_grad * unit_rows, axis=-1, keepdims=True)
        output_grad = output_grad_of(lg_ref[0], headt_ref)
        cell_low = output_grad + inv_std * (normed_grad - grad_mean - unit_rows * grad_along)
        at = lax.broadcasted_iota(jnp.int32, (WIN * WIN * 8, ROWS), 0)
        chosen = jnp.where(index_ref[0:1, :] == at, 1.0, 0.0).astype(BF16)
        placed = mm(chosen, cell_low.astype(BF16))
        placed = placed.reshape(WIN * WIN, 8, placed.shape[1])[:, :WIN].astype(BF16)
        cell[step] = placed.reshape(WIN, WIN, WIN, placed.shape[2])

    def copies(j):
        made = []
        for n, (t, x0, x1, y0, y1, to_x, to_y) in enumerate(window_pieces(windows[j])):
            made.append(
                pltpu.make_async_copy(
                    cell.at[j, x0:x1, y0:y1],
                    targets[t].at[to_x : to_x + x1 - x0, to_y : to_y + y1 - y0],
                    sems.at[j, n],
                )
            )
        return made

    @pl.when(step == 0)
    def _():
        for copy in copies(0):
            copy.start()

    @pl.when(step == 1)
    def _():
        for copy in copies(1):
            copy.start()
        for copy in copies(0) + copies(1):
            copy.wait()


def whole(shape):
    return pl.BlockSpec(shape, lambda i, *_: (0,) * len(shape))


def by_window(shape, first):
    return pl.BlockSpec((1,) + shape, lambda i, *_: (i + first,) + (0,) * len(shape))


PARAMS = pltpu.CompilerParams(vmem_limit_bytes=56 * 1024 * 1024)


def kept_shapes(width, inner):
    return [((ROWS, width), BF16), ((ROWS, 3), F32), ((ROWS, 3 * inner), BF16)]


def work_shapes(inner, width):
    heads = inner // HEAD
    return [
        pltpu.VMEM((64, 8, width + GROUP), F32),
        pltpu.VMEM((ROWS, 3 * inner), BF16),
        pltpu.VMEM((ROWS, inner), BF16),
        pltpu.VMEM((ROWS, inner), BF16),
        pltpu.VMEM((heads, LOW_ROWS, LOW_ROWS), F32),
        pltpu.VMEM((heads, HIGH_ROWS, HIGH_ROWS), F32),
        pltpu.VMEM((LOW_ROWS, LOW_ROWS), F32),
        pltpu.VMEM((HIGH_ROWS, HIGH_ROWS), F32),
    ]


def run_first(info, vol, aff, weights):
    inner, width = weights[1].shape
    kept = kept_shapes(width, inner)
    terms = [(width, 3 * inner), (width, inner)]
    return pl.pallas_call(
        first_kernel,
        name="first_window",
        grid_spec=pltpu.PrefetchScalarGridSpec(
            num_scalar_prefetch=1,
            grid=(1,),
            in_specs=[
                whole(vol.shape),
                whole(aff.shape),
                pl.BlockSpec((1, 8, 3 * GROUP), lambda i, *_: (0, 0, 0)),
                *[whole(w.shape) for w in weights],
            ],
            out_specs=[by_window(s, 0) for s, _ in kept] + [whole(s) for s in terms],
            scratch_shapes=work_shapes(inner, width),
        ),
        out_shape=[jax.ShapeDtypeStruct((4,) + s, d) for s, d in kept]
        + [jax.ShapeDtypeStruct(s, F32) for s in terms],
        compiler_params=PARAMS,
    )(info, vol, aff, jnp.asarray(source_rows()), *weights)


def run_rest(info, vol, aff, rims, weights, terms, kept_values):
    inner, width = weights[1].shape
    share = width // 16
    kept = kept_shapes(width, inner)
    return pl.pallas_call(
        rest_kernel,
        name="rest_windows",
        grid_spec=pltpu.PrefetchScalarGridSpec(
            num_scalar_prefetch=1,
            grid=(3,),
            in_specs=[
                whole(vol.shape),
                whole(aff.shape),
                *[whole(r.shape) for r in rims],
                pl.BlockSpec((1, 8, 3 * GROUP), lambda i, *_: (i + 1, 0, 0)),
                *[whole(w.shape) for w in weights],
                *[pl.BlockSpec(memory_space=pl.ANY) for _ in (*terms, *kept)],
            ],
            out_specs=[by_window(s, 1) for s, _ in kept] + [whole((4, 4, 2, share, inner))] * 2,
            scratch_shapes=[
                *[pltpu.VMEM((width, n * inner), F32) for n in (3, 1, 3, 1)],
                pltpu.SemaphoreType.DMA((2,)),
                pltpu.VMEM((ROWS, width + GROUP), F32),
            ]
            + work_shapes(inner, width),
        ),
        out_shape=[jax.ShapeDtypeStruct((4,) + s, d) for s, d in kept]
        + [
            jax.ShapeDtypeStruct((4, 4, 2, share, inner), F32),
            jax.ShapeDtypeStruct((4, 4, 2, share, inner), BF16),
        ],
        input_output_aliases={12 + i: i for i in range(3)},
        compiler_params=PARAMS,
    )(info, vol, aff, *rims, jnp.asarray(source_rows()), *weights, *terms, *kept_values)


def run_cells(windows, info, kept, wqkv, head_t, size_x, size_y, held):
    width = kept[0].shape[2]
    rest_x, rest_y = size_x - MARGIN, size_y - MARGIN
    first, change = windows[0], windows[1] - windows[0]

    def turned(shape):
        return pl.BlockSpec(
            (1,) + shape, lambda i, *_: (first + change * i,) + (0,) * len(shape)
        )

    shapes = [
        (size_x, size_y, WIN, width),
        (rest_x, MARGIN, WIN, width),
        (MARGIN, rest_y, WIN, width),
        (MARGIN, MARGIN, WIN, width),
    ]
    if held:
        shapes = [h.shape for h in held]
    anywhere = pl.BlockSpec(memory_space=pl.ANY)
    kernel = functools.partial(cell_kernel, windows, len(held))
    return pl.pallas_call(
        kernel,
        name="cell_grads",
        grid_spec=pltpu.PrefetchScalarGridSpec(
            num_scalar_prefetch=1,
            grid=(2,),
            in_specs=[
                *[turned(k.shape[1:]) for k in kept],
                whole(wqkv.shape),
                whole(head_t.shape),
                whole((8, ROWS)),
                *[anywhere for _ in held],
            ],
            out_specs=[anywhere] * len(shapes),
            scratch_shapes=[
                pltpu.VMEM((2, WIN, WIN, WIN, width), BF16),
                pltpu.SemaphoreType.DMA((2, 4)),
            ],
        ),
        out_shape=[jax.ShapeDtypeStruct(s, BF16) for s in shapes],
        input_output_aliases={7 + i: i for i in range(len(held))},
        compiler_params=PARAMS,
    )(info, *kept, wqkv, head_t, jnp.asarray(grid_rows()), *held)


def shifted(block, axes, shifts, sizes):
    first, second = sizes
    route = []
    for i in range(first):
        for j in range(second):
            to = ((i + shifts[0]) % first) * second + (j + shifts[1]) % second
            route.append((i * second + j, to))
    return lax.ppermute(block, axes, route)


def rim_message(vol, aff, rows):
    flat = jnp.concatenate([vol, aff], axis=-1)
    flat = flat.reshape(-1, flat.shape[-1])
    return jnp.pad(flat, ((0, rows - flat.shape[0]), (0, 0)))


def outgoing(total, position):
    size = total.shape[0]
    parts = []
    for shift in range(1, size):
        to = lax.rem(position + shift, size)
        parts.append(lax.dynamic_index_in_dim(total, to, 0, keepdims=False).astype(BF16))
    return parts


def incoming(total, position, got):
    mine = lax.dynamic_index_in_dim(total, position, 0, keepdims=False)
    for part in got:
        mine = mine + part.astype(F32)
    return mine


def axis_shares(total, axis, position):
    size = total.shape[0]
    got = [
        lax.ppermute(part, axis, [(i, (i + shift + 1) % size) for i in range(size)])
        for shift, part in enumerate(outgoing(total, position))
    ]
    return incoming(total, position, got)


def exchanged(parts, routes):
    return [lax.ppermute(part, "ga", route) for part, route in zip(parts, routes)]


def gathered(part, position, size):
    result = jnp.zeros((size,) + part.shape, part.dtype)
    result = lax.dynamic_update_index_in_dim(result, part, position, 0)
    for shift in range(1, size):
        got = lax.ppermute(part, "gy", [(i, (i + shift) % size) for i in range(size)])
        source = lax.rem(position + size - shift, size)
        result = lax.dynamic_update_index_in_dim(result, got, source, 0)
    return result


def per_device(volume, affinity, window_dest, qkv_weight, proj_weight, head_weight):
    size_x, size_y = volume.shape[1], volume.shape[2]
    n_gy, n_gx, n_ga = lax.axis_size("gy"), lax.axis_size("gx"), lax.axis_size("ga")
    gy, gx, ga = lax.axis_index("gy"), lax.axis_index("gx"), lax.axis_index("ga")
    m = MARGIN
    vol = volume[0]
    aff = jnp.pad(affinity[0].transpose(1, 2, 3, 0), ((0, 0), (0, 0), (0, 0), (0, GROUP - 3)))
    sizes = (n_gy, n_gx)
    axes = ("gy", "gx")

    side = shifted(rim_message(vol[m:, :m], aff[m:, :m], RIM_ROWS), axes, (0, -1), sizes)
    front = shifted(rim_message(vol[:m, m:], aff[:m, m:], RIM_ROWS), axes, (-1, 0), sizes)
    corner = shifted(rim_message(vol[:m, :m], aff[:m, :m], CORNER_ROWS), axes, (-1, -1), sizes)

    slot = lax.iota(jnp.int32, 8)
    live = jnp.pad(window_dest.reshape(-1), (0, 4))
    info = jnp.where(slot < 4, live < n_ga, False)
    info = info | ((slot == 4) & (gy == n_gy - 1)) | ((slot == 5) & (gx == n_gx - 1))
    info = (info | ((slot >= 6) & (lax.rem(ga, 2) == 1))).astype(jnp.int32)
    head_t = head_weight.T
    weights = (qkv_weight, proj_weight, head_t)

    *kept, term_q, term_p = run_first(info, vol, aff, weights)
    *kept, keep, send = run_rest(
        info, vol, aff, (side, front, corner), weights, (term_q, term_p), kept
    )
    info, send = lax.optimization_barrier((info, send))
    (got,) = exchanged([send], [[(i, i ^ 1) for i in range(n_ga)]])
    main, back_side, back_front, back_corner = run_cells(
        (3, 1), info, kept, qkv_weight, head_t, size_x, size_y, ()
    )
    total = keep + got.astype(F32)
    along = lax.div(ga, 4)
    parts = outgoing(total, along)
    info, back_side, back_corner, parts = lax.optimization_barrier(
        (info, back_side, back_corner, parts)
    )
    got = exchanged(
        parts, [[(i, (i + 4 * s) % n_ga) for i in range(n_ga)] for s in range(1, 4)]
    )
    back_side = shifted(back_side, axes, (0, 1), sizes)
    main, back_front = run_cells(
        (2, 0), info, kept, qkv_weight, head_t, size_x, size_y, (main, back_front)
    )
    total, back_front = lax.optimization_barrier((total, back_front))
    total = incoming(total, along, got)
    total = axis_shares(total, "gy", gy)
    total, back_side = lax.optimization_barrier((total, back_side))
    near = lax.rem(lax.div(ga, 2), 2)
    parts = outgoing(total, near)
    got = exchanged(parts, [[(i, i ^ 2) for i in range(n_ga)]])
    back_front = shifted(back_front, axes, (1, 0), sizes)
    back_corner = shifted(back_corner, axes, (1, 1), sizes)
    total = incoming(total, near, got)
    low = total.astype(BF16)
    for shift in range(1, n_gx):
        route = [(i, (i + shift) % n_gx) for i in range(n_gx)]
        total = total + lax.ppermute(low, "gx", route).astype(F32)
    total, back_front, back_corner = lax.optimization_barrier((total, back_front, back_corner))
    main = lax.dynamic_update_slice(main, back_side, (m, 0, 0, 0))
    main = lax.dynamic_update_slice(main, back_front, (0, m, 0, 0))
    main = lax.dynamic_update_slice(main, back_corner, (0, 0, 0, 0))
    total = total * (float(n_gy * n_gx * n_ga * 2 * WIN**3) ** (-0.5))
    parts = gathered(total, gy, n_gy)
    grad_qkv = jnp.concatenate([parts[0], parts[1], parts[2]], axis=1)
    return (main[None], grad_qkv, parts[3].T)


def solution(mesh):
    placed = (
        P("ga", "gy", "gx", None, None),
        P("ga", None, "gy", "gx", None),
        P("ga", "gy", "gx", None),
        P(),
        P(),
        P(),
    )
    return jax.shard_map(
        per_device,
        mesh=mesh,
        in_specs=placed,
        out_specs=(P("ga", "gy", "gx", None, None), P("ga", None), P(None, "ga")),
        check_vma=False,
    )
```
